32 devices in a mesh: sx: 4 (over y, x), sy: 8 (over z, core).
Axes of the slice: x: 2, y: 2, z: 4, core: 2. Of those that a mesh axis runs over, the one named last changes fastest.
Arguments:
- forward_weights: float32 [4096, 8, 432], P(('sy', 'sx')), may hold values from -6 to 6
- adjoint_weights: float32 [32768, 432], P(('sx', 'sy')), may hold values from -6 to 6
- medium: float32 [4], replicated, may hold values from 0.2 to 0.6
Outputs:
- forward_out: float32 [32768, 432], P(('sx', 'sy'))
- adjoint_out: float32 [8, 4096, 432], P(None, ('sy', 'sx'))
The draws below stay inside these ranges and needn't reach their ends.
All inputs are finite; a program needn't handle non-finite values.
Results may differ from the reference program's by a relative error of at most 0.0003.
Values sent between devices are 32-bit elements; how exact they have to be, the bound alone decides.
A program may use at most 128 MiB of HBM per device.

```python
import math
import jax
import jax.numpy as jnp
import numpy as np
from jax import lax

ORDER = 6
LEVELS = 4
TGT0 = 8
SHOTS = 1
Q = 216
SRC = 4096
TGT = 32768


def shard_levels(own_key, extent, cuts, smallest, top_value):
    level, own = 1.0, jax.random.fold_in(own_key, 6)
    for position, parts in cuts:
        heights = jnp.exp(jax.random.uniform(jax.random.fold_in(own, position), (parts,), jnp.float32, smallest / len(cuts), top_value / len(cuts)))
        level = level * jnp.repeat(heights, extent[position] // parts).reshape([-1 if axis == position else 1 for axis in range(len(extent))])
    return level


def scatter_about(key, extent, scale, bound, cuts=(), held_as=jnp.bfloat16):
    gain = shard_levels(key, extent, cuts, -0.22, 0.18) if cuts else 1.0
    entries = jax.random.normal(key, extent, jnp.float32) * scale * gain
    return jnp.minimum(jnp.maximum(entries, -bound), bound).astype(held_as)


def setup_inputs(seed: int = 0) -> dict:
    seeds = jax.random.split(jax.random.key(seed), 4)
    forward_weights = scatter_about(seeds[0], (SRC, TGT0, 2 * SHOTS * Q), 1.0, 6.0, ((0, 32),), jnp.float32)
    adjoint_weights = scatter_about(seeds[1], (TGT, 2 * SHOTS * Q), 1.0, 6.0, ((0, 32),), jnp.float32)
    medium = jnp.clip(jax.random.uniform(seeds[2], (4,), jnp.float32, 0.2, 0.6), 0.2, 0.6)
    return {"forward_weights": forward_weights, "adjoint_weights": adjoint_weights, "medium": medium}


two_pi = 2.0 * math.pi
shrink = 1.0 / math.sqrt(8.0)
band = 8.0

def cheb_points(order_count):
    return np.array([(1.0 - math.cos((2 * node_index + 1) * math.pi / (2 * order_count))) / 2.0 for node_index in range(order_count)])

def child_table(order_count):
    nodes_here = cheb_points(order_count)
    halves = []
    for offset_bit in range(2):
        matrix = np.zeros((order_count, order_count))
        for row_index in range(order_count):
            where_at = (nodes_here[row_index] + offset_bit) / 2.0
            for col_index in range(order_count):
                value_now = 1.0
                for other_index in range(order_count):
                    if other_index != col_index:
                        value_now *= (where_at - nodes_here[other_index]) / (nodes_here[col_index] - nodes_here[other_index])
                matrix[row_index, col_index] = value_now
        halves.append(matrix)
    blocks_out = []
    for child_index in range(8):
        along_x = halves[child_index // 4]
        along_y = halves[child_index // 2 % 2]
        along_z = halves[child_index % 2]
        blocks_out.append(np.kron(np.kron(along_x, along_y), along_z))
    return jnp.asarray(np.stack(blocks_out), dtype=jnp.float32)

def box_digits(box_index, groups):
    coord_x = jnp.zeros_like(box_index)
    coord_y = jnp.zeros_like(box_index)
    coord_z = jnp.zeros_like(box_index)
    for group_now in range(groups):
        digit_now = box_index // 8 ** (groups - 1 - group_now) % 8
        coord_x = coord_x * 2 + digit_now // 4
        coord_y = coord_y * 2 + digit_now // 2 % 2
        coord_z = coord_z * 2 + digit_now % 2
    return jnp.stack([coord_x, coord_y, coord_z], axis=-1).astype(jnp.float32)

def box_centres(box_index, groups):
    return (box_digits(box_index, groups) + 0.5) / float(2 ** groups)

def box_points(box_index, groups):
    box_side = band / float(2 ** groups)
    nodes_here = jnp.asarray(cheb_points(ORDER), dtype=jnp.float32)
    grid_x = jnp.repeat(nodes_here, ORDER * ORDER)
    grid_y = jnp.tile(jnp.repeat(nodes_here, ORDER), ORDER)
    grid_z = jnp.tile(nodes_here, ORDER * ORDER)
    offsets = jnp.stack([grid_x, grid_y, grid_z], axis=-1)
    corner = box_digits(box_index, groups)
    return box_side * (corner[..., None, :] + offsets)

def phase_angle(centres, points, medium):
    along = lax.optimization_barrier(jnp.sum(centres * points, axis=-1))
    radius = jnp.sqrt(lax.optimization_barrier(jnp.sum(points * points, axis=-1)))
    travel = medium[0] + lax.optimization_barrier(jnp.sum(medium[1:] * centres, axis=-1))
    return two_pi * (along + travel * radius)

def complex_turn(real_part, imag_part, angle_now, sign_now):
    cosine = jnp.cos(angle_now)
    sine_part = sign_now * jnp.sin(angle_now)
    return (real_part * cosine - imag_part * sine_part, real_part * sine_part + imag_part * cosine)

def forward_level(weights, src_off, tgt_off, level_now, medium, interp):
    src_count, tgt_count = (weights.shape[0], weights.shape[1])
    shot_count, point_count = (weights.shape[3], weights.shape[4])
    parent_count = src_count // 8
    new_targets = tgt_off * 8 + jnp.arange(tgt_count * 8, dtype=jnp.int32)
    centres = box_centres(new_targets, level_now + 2).reshape(tgt_count, 8, 3)
    children = src_off + jnp.arange(src_count, dtype=jnp.int32)
    child_points = box_points(children, LEVELS - level_now).reshape(parent_count, 8, point_count, 3)
    parents = src_off // 8 + jnp.arange(parent_count, dtype=jnp.int32)
    parent_points = box_points(parents, LEVELS - level_now - 1)
    theta_in = phase_angle(centres[None, None, :, :, None, :], child_points[:, :, None, None, :, :], medium)
    theta_out = phase_angle(centres[None, :, :, None, :], parent_points[:, None, None, :, :], medium)
    shaped = weights.reshape(parent_count, 8, tgt_count, 1, 2, shot_count, point_count)
    turned = complex_turn(shaped[:, :, :, :, 0], shaped[:, :, :, :, 1], theta_in[:, :, :, :, None, :], 1.0)
    stacked = jnp.stack(turned, axis=4)
    mixed = jnp.einsum('pctkxhq,cqs->ptkxhs', stacked, interp, precision=lax.Precision.HIGHEST)
    result_re, result_im = complex_turn(mixed[:, :, :, 0], mixed[:, :, :, 1], theta_out[:, :, :, None, :], -1.0)
    output = shrink * jnp.stack([result_re, result_im], axis=3)
    return output.reshape(parent_count, tgt_count * 8, 2, shot_count, point_count)

def adjoint_level(values, tgt_off, src_off, level_now, medium, interp):
    tgt_count, src_count = (values.shape[0], values.shape[1])
    shot_count, point_count = (values.shape[3], values.shape[4])
    parent_count = tgt_count // 8
    targets = tgt_off + jnp.arange(tgt_count, dtype=jnp.int32)
    centres = box_centres(targets, level_now + 2).reshape(parent_count, 8, 3)
    sources = src_off + jnp.arange(src_count, dtype=jnp.int32)
    source_points = box_points(sources, LEVELS - level_now - 1)
    children = src_off * 8 + jnp.arange(src_count * 8, dtype=jnp.int32)
    child_points = box_points(children, LEVELS - level_now).reshape(src_count, 8, point_count, 3)
    theta_out = phase_angle(centres[:, :, None, None, :], source_points[None, None, :, :, :], medium)
    theta_in = phase_angle(centres[:, :, None, None, None, :], child_points[None, None, :, :, :, :], medium)
    shaped = values.reshape(parent_count, 8, src_count, 2, shot_count, point_count)
    turned = complex_turn(shaped[:, :, :, 0], shaped[:, :, :, 1], theta_out[:, :, :, None, :], 1.0)
    stacked = jnp.stack(turned, axis=3)
    spread = jnp.einsum('pkbxhs,cqs->pkbcxhq', stacked, interp, precision=lax.Precision.HIGHEST)
    back_re, back_im = complex_turn(spread[:, :, :, :, 0], spread[:, :, :, :, 1], theta_in[:, :, :, :, None, :], -1.0)
    output = shrink * jnp.stack([lax.optimization_barrier(jnp.sum(back_re, axis=1)), lax.optimization_barrier(jnp.sum(back_im, axis=1))], axis=3)
    return output.reshape(parent_count, src_count * 8, 2, shot_count, point_count)

def blocked(level_fn, array_in):
    first_size, second_size = (array_in.shape[0], array_in.shape[1])
    block_ids = jnp.arange(8, dtype=jnp.int32)
    if first_size >= second_size:
        pieces = array_in.reshape((8, first_size // 8) + array_in.shape[1:])
        results = lax.map(lambda packed: level_fn(packed[0], packed[1] * (first_size // 8), jnp.int32(0)), (pieces, block_ids))
        return results.reshape((results.shape[0] * results.shape[1],) + results.shape[2:])
    pieces = jnp.swapaxes(array_in.reshape((first_size, 8, second_size // 8) + array_in.shape[2:]), 0, 1)
    results = lax.map(lambda packed: level_fn(packed[0], jnp.int32(0), packed[1] * (second_size // 8)), (pieces, block_ids))
    results = jnp.swapaxes(results, 0, 1)
    return results.reshape((results.shape[0], results.shape[1] * results.shape[2]) + results.shape[3:])

def reference(forward_weights, adjoint_weights, medium):
    interp = child_table(ORDER)
    current = forward_weights.reshape(forward_weights.shape[0], forward_weights.shape[1], 2, -1, Q)
    for level_now in range(LEVELS):
        current = blocked(lambda block_now, first_off, second_off: forward_level(block_now, first_off, second_off, level_now, medium, interp), current)
    forward_out = current.reshape(current.shape[1], -1)
    current = adjoint_weights.reshape(adjoint_weights.shape[0], 1, 2, -1, Q)
    for level_now in reversed(range(LEVELS)):
        current = blocked(lambda block_now, first_off, second_off: adjoint_level(block_now, first_off, second_off, level_now, medium, interp), current)
    adjoint_out = current.reshape(current.shape[0], current.shape[1], -1)
    return (forward_out, adjoint_out)
```

```python
import math

import jax
import jax.numpy as jnp
import ml_dtypes
import numpy as np
from jax import lax
from jax.experimental import pallas as pl
from jax.experimental.pallas import tpu as pltpu
from jax.sharding import PartitionSpec as P

ORDER = 6
LEVELS = 4
Q = 216
band = 8.0


def cheb_points(n):
    return np.array([(1.0 - math.cos((2 * i + 1) * math.pi / (2 * n))) / 2.0 for i in range(n)])


def child_table(n):
    g = cheb_points(n)
    halves = []
    for bit in range(2):
        m = np.ones((n, n))
        for r in range(n):
            w = (g[r] + bit) / 2.0
            for c in range(n):
                for o in range(n):
                    if o != c:
                        m[r, c] *= (w - g[o]) / (g[c] - g[o])
        halves.append(m)
    return np.stack(
        [np.kron(np.kron(halves[e // 4], halves[e // 2 % 2]), halves[e % 2]) for e in range(8)]
    )


def split_table(table):
    high = table.astype(ml_dtypes.bfloat16)
    low = (table - high.astype(np.float64)).astype(ml_dtypes.bfloat16)
    return jnp.asarray(high), jnp.asarray(low)


def box_coords(index, groups):
    coords = [jnp.zeros_like(index) for _ in range(3)]
    for group in range(groups):
        digit = index // 8 ** (groups - 1 - group) % 8
        bits = (digit // 4, digit // 2 % 2, digit % 2)
        coords = [c * 2 + b for c, b in zip(coords, bits)]
    return [c.astype(jnp.float32) for c in coords]


def point_slopes(src_off, count, groups, medium):
    side = band / float(2**groups)
    g = cheb_points(ORDER).astype(np.float32)
    grid = (np.repeat(g, ORDER * ORDER), np.tile(np.repeat(g, ORDER), ORDER), np.tile(g, ORDER**2))
    corner = box_coords(src_off + jnp.arange(count, dtype=jnp.int32), groups)
    pts = [side * (c[:, None] + o[None, :]) for c, o in zip(corner, grid)]
    radius = jnp.sqrt(pts[0] * pts[0] + pts[1] * pts[1] + pts[2] * pts[2])
    return [p + medium[d + 1] * radius for d, p in enumerate(pts)], medium[0] * radius


def turn_of(u):
    half = jnp.round(2.0 * u)
    y = (2.0 * math.pi) * (u - 0.5 * half)
    sign = 1.0 - 2.0 * (half - 2.0 * jnp.floor(0.5 * half))
    z = y * y
    s = jnp.float32(-1.0 / math.factorial(11))
    for n in (9, 7, 5, 3, 1):
        s = s * z + (1.0 if n % 4 == 1 else -1.0) / math.factorial(n)
    c = jnp.float32(1.0 / math.factorial(12))
    for n in (10, 8, 6, 4, 2, 0):
        c = c * z + (1.0 if n % 4 == 0 else -1.0) / math.factorial(n)
    return sign * c, sign * (s * y)


def pair_phase(src_off, src_count, src_groups, tgt_off, tgt_count, tgt_groups, medium):
    slopes, base = point_slopes(src_off, src_count, src_groups, medium)
    coords = box_coords(tgt_off + jnp.arange(tgt_count, dtype=jnp.int32), tgt_groups)
    u = base[:, None, :]
    for c, a in zip(coords, slopes):
        u = u + ((c + 0.5) / float(2**tgt_groups))[None, :, None] * a[:, None, :]
    return turn_of(u)


def child_phase(src_off, src_count, level, medium):
    slopes, _ = point_slopes(src_off, src_count, LEVELS - level, medium)
    k = np.arange(8)
    u = 0.0
    for bits, a in zip((k // 4, k // 2 % 2, k % 2), slopes):
        step = ((bits - 0.5) / 2.0 ** (level + 2)).astype(np.float32)
        u = u + step[None, :, None] * a[:, None, :]
    return jnp.stack(turn_of(u), axis=1)


def dot3(x, high, low):
    x_high = x.astype(jnp.bfloat16)
    x_low = (x - x_high.astype(jnp.float32)).astype(jnp.bfloat16)
    dot = lambda a, b: jnp.dot(a, b, preferred_element_type=jnp.float32)
    return dot(x_high, high) + dot(x_high, low) + dot(x_low, high)


def forward_kernel(x_ref, w_ref, high_ref, low_ref, o_ref):
    pb, _, _, tb, q = o_ref.shape[0], 2, 8, o_ref.shape[3], o_ref.shape[4]

    def step(e, acc):
        parts = []
        for p in range(pb):
            re, im = x_ref[p, e, 0], x_ref[p, e, 1]
            w_re, w_im = w_ref[p, e, 0], w_ref[p, e, 1]
            res = [re * w_re[k : k + 1] - im * w_im[k : k + 1] for k in range(8)]
            ims = [re * w_im[k : k + 1] + im * w_re[k : k + 1] for k in range(8)]
            parts += res + ims
        return acc + dot3(jnp.concatenate(parts, axis=0), high_ref[e], low_ref[e])

    acc = lax.fori_loop(0, 8, step, jnp.zeros((pb * 16 * tb, q), jnp.float32))
    o_ref[...] = acc.reshape(o_ref.shape)


def adjoint_kernel(y_ref, w_ref, high_ref, low_ref, o_ref):
    sb, tb, q = y_ref.shape[0], y_ref.shape[3], y_ref.shape[4]
    rows = y_ref[...].reshape(sb * 16 * tb, q)

    def step(e, carry):
        z = dot3(rows, high_ref[e], low_ref[e]).reshape(sb, 2, 8, tb, q)
        for s in range(sb):
            w_re, w_im = w_ref[s, e, 0], w_ref[s, e, 1]
            out_re = jnp.zeros((tb, q), jnp.float32)
            out_im = jnp.zeros((tb, q), jnp.float32)
            for k in range(8):
                re, im = z[s, 0, k], z[s, 1, k]
                c, d = w_re[k : k + 1], w_im[k : k + 1]
                out_re += re * c + im * d
                out_im += im * c - re * d
            o_ref[s, e, 0] = out_re
            o_ref[s, e, 1] = out_im
        return carry

    lax.fori_loop(0, 8, step, 0)


def blocks(count, tgt):
    tb = min(tgt, 32)
    return math.gcd(count, max(1, 32 // tb)), tb


def level_call(kernel, operand, phase, tables, out_shape):
    count, tgt, q = operand.shape[0], operand.shape[3], operand.shape[4]
    cb, tb = blocks(count, tgt)
    spec = lambda: pl.BlockSpec((cb, operand.shape[1], operand.shape[2], tb, q), lambda i, j: (i, 0, 0, j, 0))
    return pl.pallas_call(
        kernel,
        grid=(count // cb, tgt // tb),
        in_specs=[
            spec(),
            pl.BlockSpec((cb,) + phase.shape[1:], lambda i, j: (i, 0, 0, 0, 0)),
            pl.BlockSpec(tables[0].shape, lambda i, j: (0, 0, 0)),
            pl.BlockSpec(tables[1].shape, lambda i, j: (0, 0, 0)),
        ],
        out_specs=pl.BlockSpec((cb, out_shape[1], out_shape[2], tb, q), lambda i, j: (i, 0, 0, j, 0)),
        out_shape=jax.ShapeDtypeStruct(out_shape, jnp.float32),
        compiler_params=pltpu.CompilerParams(vmem_limit_bytes=56 * 1024 * 1024),
    )(operand, phase, *tables)


def forward_level(x, src_off, level, medium, tables):
    count, _, tgt, q = x.shape
    phase = child_phase(src_off, count, level, medium).reshape(count // 8, 8, 2, 8, q)
    out = level_call(
        forward_kernel, x.reshape(count // 8, 8, 2, tgt, q), phase, tables, (count // 8, 2, 8, tgt, q)
    )
    return out.swapaxes(2, 3).reshape(count // 8, 2, tgt * 8, q)


def adjoint_level(y, src_off, level, medium, tables):
    count, _, tgt, q = y.shape
    phase = child_phase(src_off * 8, count * 8, level, medium).reshape(count, 8, 2, 8, q)
    operand = y.reshape(count, 2, tgt // 8, 8, q).swapaxes(2, 3)
    out = level_call(adjoint_kernel, operand, phase, tables, (count, 8, 2, tgt // 8, q))
    return out.reshape(count * 8, 2, tgt // 8, q)


def shards(forward_weights, adjoint_weights, medium):
    table = child_table(ORDER) / math.sqrt(8.0)
    forward_tables = split_table(table)
    adjoint_tables = split_table(table.transpose(0, 2, 1))
    sizes = {a: lax.axis_size(a) for a in ("sx", "sy")}
    index = {a: lax.axis_index(a) for a in ("sx", "sy")}
    local_sources = forward_weights.shape[0]
    shots = forward_weights.shape[2] // (2 * Q)
    plan = []
    remaining = ["sx", "sy"]
    width = local_sources
    for _ in range(LEVELS):
        while width < 8:
            axis = remaining.pop(0)
            plan.append(axis)
            width *= sizes[axis]
        plan.append("level")
        width //= 8

    f_in = forward_weights.reshape(local_sources, -1, 2, shots, Q)
    b_in = adjoint_weights.reshape(adjoint_weights.shape[0], 2, shots, Q)
    f_src = (index["sy"] * sizes["sx"] + index["sx"]) * local_sources
    b_tgt = (index["sx"] * sizes["sy"] + index["sy"]) * adjoint_weights.shape[0]
    f_outs, b_outs = [], []
    for shot in range(shots):
        src, tgt, level = f_src, jnp.int32(0), 0
        re, im = f_in[:, :, 0, shot], f_in[:, :, 1, shot]
        c, s = pair_phase(src, re.shape[0], LEVELS, tgt, re.shape[1], 1, medium)
        x = jnp.stack([re * c - im * s, re * s + im * c], axis=1)
        for op in plan:
            if op == "level":
                x = forward_level(x, src, level, medium, forward_tables)
                src, tgt, level = src // 8, tgt * 8, level + 1
            else:
                n = sizes[op]
                count, _, width, _ = x.shape
                x = x.reshape(count, 2, n, width // n, Q).transpose(2, 0, 1, 3, 4)
                x = lax.all_to_all(x, op, split_axis=0, concat_axis=0, tiled=True)
                x = x.reshape(n * count, 2, width // n, Q)
                src = src - index[op] * count
                tgt = tgt + index[op] * (width // n)
        c, s = pair_phase(src, x.shape[0], LEVELS - level, tgt, x.shape[2], level + 1, medium)
        re, im = x[:, 0], x[:, 1]
        f_outs.append((re * c + im * s, im * c - re * s))
        src, tgt, level = jnp.int32(0), b_tgt, LEVELS
        re, im = b_in[None, :, 0, shot], b_in[None, :, 1, shot]
        c, s = pair_phase(src, 1, 0, tgt, re.shape[1], LEVELS + 1, medium)
        y = jnp.stack([re * c - im * s, re * s + im * c], axis=1)
        for op in reversed(plan):
            if op == "level":
                y = adjoint_level(y, src, level - 1, medium, adjoint_tables)
                src, tgt, level = src * 8, tgt // 8, level - 1
            else:
                n = sizes[op]
                count, _, width, _ = y.shape
                y = y.reshape(n, count // n, 2, width, Q)
                y = lax.all_to_all(y, op, split_axis=0, concat_axis=0, tiled=True)
                y = y.transpose(1, 2, 0, 3, 4).reshape(count // n, 2, n * width, Q)
                src = src + index[op] * (count // n)
                tgt = tgt - index[op] * width
        c, s = pair_phase(src, y.shape[0], LEVELS, tgt, y.shape[2], 1, medium)
        re, im = y[:, 0], y[:, 1]
        b_outs.append((re * c + im * s, im * c - re * s))
    f = jnp.stack([jnp.stack([o[i][0] for o in f_outs], axis=1) for i in range(2)], axis=1)
    b = jnp.stack([jnp.stack([o[i].swapaxes(0, 1) for o in b_outs], axis=2) for i in range(2)], axis=2)
    return f.reshape(f.shape[0], -1), b.reshape(b.shape[0], b.shape[1], -1)


def solution(mesh):
    in_specs = (P(("sy", "sx"), None, None), P(("sx", "sy"), None), P())
    out_specs = (P(("sx", "sy"), None), P(None, ("sy", "sx"), None))
    return jax.shard_map(shards, mesh=mesh, in_specs=in_specs, out_specs=out_specs, check_vma=False)
```
